32 devices in a mesh: win: 16 (over z, y, x), head: 2 (over core).
Axes of the slice: x: 2, y: 2, z: 4, core: 2. Of those that a mesh axis runs over, the one named last changes fastest.
Arguments:
- coords: float32 [3, 512, 128], P(None, 'win', 'head'), may hold values from -8 to 16
- noise: float32 [3, 512, 128], P(None, 'win', 'head'), may hold values from -6 to 6
- sigma: float32 [1], replicated, may hold values from 0.25 to 1
- atom_single: bfloat16 [512, 128, 128], P('win', 'head'), may hold values from -6 to 6
- token_single: bfloat16 [8192, 384], P('win'), may hold values from -6 to 6
- atom_token: int32 [512, 128], P('win', 'head'), may hold values from 0 to 15, never falling along the last dimension, each value on 1 to 64 neighbouring positions
- window_count: int32 [16], replicated, may hold values from 1 to 31, as said below
- pair_bias: bfloat16 [4, 512, 128, 128], P('head', 'win'), may hold values from -6 to 260
- token_weight: bfloat16 [384, 128], replicated, may hold values from -0.3125 to 0.3125
- cond_gain: float32 [128], replicated, may hold values from 0.25 to 1.75
- position_weight: float32 [3, 128], replicated, may hold values from -3.5 to 3.5
- ada_weight: bfloat16 [3, 6, 128, 128], replicated, may hold values from -0.5 to 0.5
- ada_bias: float32 [3, 6, 128], replicated, may hold values from -4 to 4
- attn_weight: bfloat16 [3, 4, 128, 128], P(None, None, None, 'head'), may hold values from -0.5 to 0.5
- out_weight: bfloat16 [3, 128, 128], P(None, 'head'), may hold values from -0.5 to 0.5
- gateup_weight: bfloat16 [3, 2, 128, 256], replicated, may hold values from -0.5 to 0.5
- down_weight: bfloat16 [3, 256, 128], replicated, may hold values from -0.375 to 0.375
- final_weight: bfloat16 [3, 128], replicated, may hold values from -0.5 to 0.5
Outputs:
- denoised: float32 [3, 512, 128], P(None, 'win', 'head')
The draws below stay inside these ranges and needn't reach their ends.
Inputs may be any that keep to these rules, and one draw needn't show every extreme that they name: window_count[d] + window_count[d + 8] <= 32 for every d < 8, with equality for some d.
All inputs are finite; a program needn't handle non-finite values.
Results may differ from the reference program's by a relative error of at most 0.005.
Values may be sent and summed in bfloat16 or wider, within the bound.
No kernel may reach another device: no remote copies, remote signals or barrier semaphores. Data moves between devices by JAX's collectives and lax.ppermute only.
A program may use at most 128 MiB of HBM per device.

```python
import math
import jax
import jax.numpy as jnp
import numpy as np
from jax import lax

C = 128
HEADS = 4
HEAD_DIM = 32
HID = 256
C_S = 384
QW = 128
TOKW = 16
BLOCKS = 3
WIN_DEV = 32
TOK_DEV = 512
WINDOWS = 512
TOKENS = 8192
N_WIN = 16


def draw_coords(key, part):
    first_key = jax.random.fold_in(jax.random.fold_in(key, 11), 0)
    along = jnp.arange(WINDOWS, dtype=jnp.float32) / WINDOWS
    component = (jnp.arange(3) == 0).astype(jnp.float32)
    rough = jnp.clip(jax.random.normal(first_key, (3, WINDOWS, QW), jnp.float32), -4.0, 4.0)
    offset = 2.0 + 4.0 * along
    return rough + component[:, None, None] * offset[None, :, None]


def draw_window_count(key, part):
    half_count = N_WIN // 2
    first_key, second_key, third_key = jax.random.split(jax.random.fold_in(key, 23), 3)
    positions = jnp.arange(half_count, dtype=jnp.int32)
    first_count = jax.random.randint(first_key, (half_count,), 1, WIN_DEV, dtype=jnp.int32)
    first_count = jnp.where(positions == 0, WIN_DEV - 1, first_count)
    room_left = WIN_DEV - first_count
    second_count = 1 + jax.random.randint(second_key, (half_count,), 0, 1048576, dtype=jnp.int32) % room_left
    second_count = jnp.where(positions == 0, room_left, second_count)
    flipped = jax.random.randint(third_key, (half_count,), 0, 2, dtype=jnp.int32)
    lower_half = jnp.where(flipped == 1, second_count, first_count)
    upper_half = jnp.where(flipped == 1, first_count, second_count)
    return jnp.concatenate([lower_half, upper_half]).astype(jnp.int32)


def draw_pair_bias(key, part):
    first_key = jax.random.fold_in(jax.random.fold_in(key, 37), 0)
    shape_all = (HEADS, WINDOWS, QW, QW)
    base = jnp.clip(jax.random.normal(first_key, shape_all, jnp.float32), -6.0, 6.0)
    return base.astype(jnp.bfloat16)


def block_scale(stream_key, dims, shards, smallest, high):
    gain, own = 1.0, jax.random.fold_in(stream_key, 6)
    for dim, blocks in shards:
        heights = jnp.exp(jax.random.uniform(jax.random.fold_in(own, dim), (blocks,), jnp.float32, smallest / len(shards), high / len(shards)))
        gain = gain * jnp.repeat(heights, dims[dim] // blocks).reshape([-1 if axis == dim else 1 for axis in range(len(dims))])
    return gain


def profile(number_of, total, bound, skew):
    portions = [(1 << 20) // math.isqrt(rank ** skew) + 1 for rank in range(2, number_of + 1)]
    rest, given = total - bound - (number_of - 1), [1] * (number_of - 1)
    while rest > 0:
        candidates = [i for i in range(number_of - 1) if given[i] < bound]
        mass, remaining = sum([portions[i] for i in candidates]), rest
        for i in candidates:
            extra = min(bound - given[i], max(1, remaining * portions[i] // mass), rest)
            given[i] = given[i] + extra
            rest = rest - extra
    return np.array([bound] + given)


def uneven(stream_key, amount, total, limit, slope):
    if amount == 2:
        one = jax.random.randint(stream_key, (), max(1, total - limit), min(limit, total - 1) + 1)
        return jnp.stack([one, total - one])
    lengths = jnp.asarray(profile(amount, total, limit, slope), jnp.int32)
    pairs = (amount - 1) // 2
    donor, taker = lengths[1:1 + 2 * pairs:2], lengths[2:2 + 2 * pairs:2]
    room = jnp.minimum(donor - 1, limit - taker)
    passed = jax.random.randint(jax.random.fold_in(stream_key, 1), (pairs,), 0, 1 << 20) % (room + 1)
    lengths = lengths.at[1:1 + 2 * pairs:2].set(donor - passed).at[2:2 + 2 * pairs:2].set(taker + passed)
    return lengths[jax.random.permutation(jax.random.fold_in(stream_key, 2), amount)]


def bell_draw(key, dims, spread, bound, cuts=(), kind=jnp.bfloat16):
    loudness = block_scale(key, dims, cuts, -0.22, 0.18) if cuts else 1.0
    values = jax.random.normal(key, dims, jnp.float32) * spread * loudness
    return jnp.minimum(jnp.maximum(values, -bound), bound).astype(kind)


def setup_inputs(seed: int = 0) -> dict:
    key_list = jax.random.split(jax.random.key(seed), 19)
    coords = draw_coords(jax.random.fold_in(key_list[18], 71), 0)
    noise = bell_draw(key_list[1], (3, WINDOWS, QW), 1.0, 6.0, ((1, 16), (2, 2)), jnp.float32)
    sigma = jnp.clip(jnp.exp(jax.random.uniform(key_list[2], (1,), jnp.float32, math.log(0.25), math.log(1.0))), 0.25, 1.0)
    atom_single = bell_draw(key_list[3], (WINDOWS, QW, C), 1.0, 6.0, ((0, 16), (1, 2)))
    token_single = bell_draw(key_list[4], (TOKENS, C_S), 1.0, 6.0, ((0, 16),))
    atom_token = jax.vmap(lambda own: jnp.searchsorted(jnp.cumsum(uneven(own, TOKW, QW, QW // 2, 2)), jnp.arange(QW), side="right"))(jax.random.split(key_list[5], WINDOWS)).reshape((WINDOWS, QW)).astype(jnp.int32)
    window_count = draw_window_count(jax.random.fold_in(key_list[18], 71), 0)
    pair_bias = draw_pair_bias(jax.random.fold_in(key_list[18], 71), 0)
    token_weight = bell_draw(key_list[8], (C_S, C), C_S ** -0.5, 0.3125)
    cond_gain = jnp.clip(1.0 + 0.15 * jax.random.normal(key_list[9], (C,), jnp.float32), 0.25, 1.75)
    position_weight = bell_draw(key_list[10], (3, C), 3 ** -0.5, 3.5, (), jnp.float32)
    ada_weight = bell_draw(key_list[11], (BLOCKS, 6, C, C), C ** -0.5, 0.5)
    ada_bias = bell_draw(key_list[12], (BLOCKS, 6, C), 1.0, 4.0, (), jnp.float32)
    attn_weight = bell_draw(key_list[13], (BLOCKS, 4, C, C), C ** -0.5, 0.5, ((3, 2),))
    out_weight = bell_draw(key_list[14], (BLOCKS, C, C), C ** -0.5, 0.5, ((1, 2),))
    gateup_weight = bell_draw(key_list[15], (BLOCKS, 2, C, HID), C ** -0.5, 0.5)
    down_weight = bell_draw(key_list[16], (BLOCKS, HID, C), HID ** -0.5, 0.375)
    final_weight = bell_draw(key_list[17], (3, C), C ** -0.5, 0.5)
    return {"coords": coords, "noise": noise, "sigma": sigma, "atom_single": atom_single, "token_single": token_single, "atom_token": atom_token, "window_count": window_count, "pair_bias": pair_bias, "token_weight": token_weight, "cond_gain": cond_gain, "position_weight": position_weight, "ada_weight": ada_weight, "ada_bias": ada_bias, "attn_weight": attn_weight, "out_weight": out_weight, "gateup_weight": gateup_weight, "down_weight": down_weight, "final_weight": final_weight}


EPSILON = 1e-05

def layer_norm(values):
    average = lax.optimization_barrier(jnp.mean(values, axis=-1, keepdims=True))
    centred = values - average
    variance = lax.optimization_barrier(jnp.mean(centred * centred, axis=-1, keepdims=True))
    return centred * lax.rsqrt(variance + EPSILON)

def lookup_tokens(tokens_here, local_token):
    token_grid = tokens_here.reshape(local_token.shape[0], TOKW, -1).astype(jnp.float32)
    one_hot = (local_token[:, :, None] == jnp.arange(TOKW, dtype=jnp.int32)).astype(jnp.float32)
    return jnp.einsum('wqt,wtc->wqc', one_hot, token_grid).astype(jnp.bfloat16)

def window_net(single, looked, scaled, pair_terms, weights_all):
    cond_gain, position_weight, ada_weight, ada_bias, attn_weight, out_weight, gateup_weight, down_weight, final_weight = weights_all
    condition = single.astype(jnp.float32) + looked.astype(jnp.float32)
    cond_norm = (layer_norm(condition) * cond_gain).astype(jnp.bfloat16)
    stream = condition + jnp.einsum('kwq,kc->wqc', scaled, position_weight, precision=lax.Precision.HIGHEST)
    window_total, row_count = (single.shape[0], single.shape[1])
    for block_index in range(BLOCKS):
        ada_terms = jnp.einsum('wqc,jcd->jwqd', cond_norm.astype(jnp.float32), ada_weight[block_index].astype(jnp.float32)) + ada_bias[block_index][:, None, None, :]
        normed = (layer_norm(stream) * jax.nn.sigmoid(ada_terms[0]) + ada_terms[1]).astype(jnp.bfloat16)
        projected = jnp.einsum('wqc,jcd->jwqd', normed.astype(jnp.float32), attn_weight[block_index].astype(jnp.float32)).astype(jnp.bfloat16)
        query_rows = projected[0].reshape(window_total, row_count, -1, HEAD_DIM).astype(jnp.float32)
        key_rows = projected[1].reshape(window_total, row_count, -1, HEAD_DIM).astype(jnp.float32)
        value_rows = projected[2].reshape(window_total, row_count, -1, HEAD_DIM).astype(jnp.float32)
        gate_logits = projected[3].reshape(window_total, row_count, -1, HEAD_DIM).astype(jnp.float32)
        scores = jnp.einsum('wqhd,wkhd->hwqk', query_rows, key_rows) * HEAD_DIM ** (-0.5) + pair_terms.astype(jnp.float32)
        row_max = lax.optimization_barrier(jnp.max(scores, axis=-1, keepdims=True))
        exponent = jnp.exp(scores - row_max)
        weights = (exponent / lax.optimization_barrier(jnp.sum(exponent, axis=-1, keepdims=True))).astype(jnp.bfloat16)
        attended = jnp.einsum('hwqk,wkhd->wqhd', weights.astype(jnp.float32), value_rows) * jax.nn.sigmoid(gate_logits)
        attended = attended.astype(jnp.bfloat16).reshape(window_total, row_count, -1)
        update = jnp.einsum('wqd,dc->wqc', attended.astype(jnp.float32), out_weight[block_index].astype(jnp.float32))
        stream = stream + jax.nn.sigmoid(ada_terms[2]) * update
        normed_two = (layer_norm(stream) * jax.nn.sigmoid(ada_terms[3]) + ada_terms[4]).astype(jnp.bfloat16)
        gate_part = jnp.einsum('wqc,ch->wqh', normed_two.astype(jnp.float32), gateup_weight[block_index, 0].astype(jnp.float32))
        up_part = jnp.einsum('wqc,ch->wqh', normed_two.astype(jnp.float32), gateup_weight[block_index, 1].astype(jnp.float32))
        hidden = (jax.nn.silu(gate_part) * up_part).astype(jnp.bfloat16)
        down_part = jnp.einsum('wqh,hc->wqc', hidden.astype(jnp.float32), down_weight[block_index].astype(jnp.float32))
        stream = stream + jax.nn.sigmoid(ada_terms[5]) * down_part
    final_norm = layer_norm(stream).astype(jnp.bfloat16)
    return jnp.einsum('wqc,kc->kwq', final_norm.astype(jnp.float32), final_weight.astype(jnp.float32))

def reference(coords, noise, sigma, atom_single, token_single, atom_token, window_count, pair_bias, token_weight, cond_gain, position_weight, ada_weight, ada_bias, attn_weight, out_weight, gateup_weight, down_weight, final_weight):
    sigma_value = sigma[0]
    noisy_pos = coords + sigma_value * noise
    slot_ids = jnp.arange(WINDOWS, dtype=jnp.int32) % WIN_DEV
    block_ids = jnp.arange(WINDOWS, dtype=jnp.int32) // WIN_DEV
    live_mask = (slot_ids < window_count[block_ids]).astype(jnp.float32)
    totals = lax.optimization_barrier(jnp.sum(noisy_pos * live_mask[None, :, None], axis=(1, 2)))
    centre = totals / (QW * jnp.sum(window_count).astype(jnp.float32))
    shifted = noisy_pos - centre[:, None, None]
    inverse = 1.0 / (1.0 + sigma_value * sigma_value)
    scaled = shifted * jnp.sqrt(inverse)
    token_proj = jnp.dot(token_single, token_weight, preferred_element_type=jnp.float32).astype(jnp.bfloat16)
    weights_all = (cond_gain, position_weight, ada_weight, ada_bias, attn_weight, out_weight, gateup_weight, down_weight, final_weight)

    def one_group(group_index):
        first_window = group_index * WIN_DEV
        single = lax.dynamic_slice_in_dim(atom_single, first_window, WIN_DEV, 0)
        tokens_here = lax.dynamic_slice_in_dim(token_proj, group_index * TOK_DEV, TOK_DEV, 0)
        local_token = lax.dynamic_slice_in_dim(atom_token, first_window, WIN_DEV, 0)
        scaled_here = lax.dynamic_slice_in_dim(scaled, first_window, WIN_DEV, 1)
        pair_terms = lax.dynamic_slice_in_dim(pair_bias, first_window, WIN_DEV, 1)
        looked = lookup_tokens(tokens_here, local_token)
        return window_net(single, looked, scaled_here, pair_terms, weights_all)
    updates = lax.map(one_group, jnp.arange(N_WIN, dtype=jnp.int32))
    update_pos = jnp.moveaxis(updates, 1, 0).reshape(3, WINDOWS, QW)
    denoised = shifted * inverse + sigma_value * jnp.sqrt(inverse) * update_pos
    return denoised * live_mask[None, :, None]
```

```python
import functools

import jax
import jax.numpy as jnp
from jax import lax
from jax.experimental import pallas as pl
from jax.experimental.pallas import tpu as pltpu
from jax.sharding import PartitionSpec as P

HEAD_DIM = 32
QW = 128
TOKW = 16
BLOCKS = 3
HEADS = 4
GROUP = 4

EPSILON = 1e-05
F32 = jnp.float32
BF16 = jnp.bfloat16


def dot(left, right):
    return jnp.dot(left, right, preferred_element_type=F32)


def dot_nt(left, right):
    return lax.dot_general(left, right, (((1,), (1,)), ((), ())), preferred_element_type=F32)


def eye(size):
    rows = lax.broadcasted_iota(jnp.int32, (size, size), 0)
    columns = lax.broadcasted_iota(jnp.int32, (size, size), 1)
    return jnp.where(rows == columns, 1.0, 0.0).astype(BF16)


def split(value):
    high = value.astype(BF16).astype(F32)
    rest = value - high
    middle = rest.astype(BF16).astype(F32)
    return high, middle, rest - middle


def centred(values):
    average = jnp.mean(values, axis=0, keepdims=True)
    rest = values - average
    variance = jnp.mean(rest * rest, axis=0, keepdims=True)
    return rest, lax.rsqrt(variance + EPSILON)


def prepare(
    weights, ada_t, attn_t, out_t, gateup_t, down_t, token_t, position_l, gain_b
):
    (ada, ada_bias, attn_own, attn_other, out_own, out_other, gateup, down, token, position, gain) = weights
    one = eye(QW)
    small = eye(QW // 2)

    def block(b, carry):
        for j in range(6):
            factor = 1.0 if j in (1, 4) else 0.5
            bias = ada_bias[b, pl.ds(j, 1), :]
            high, middle, low = split(bias)
            pad = jnp.zeros((7, QW), F32)
            tail = jnp.concatenate(
                [high, pad, middle, pad, low, pad, jnp.zeros((QW - 24, QW), F32)], axis=0
            ).astype(BF16)
            whole = jnp.concatenate([ada[b, j], tail], axis=0)
            ada_t[b, pl.ds(j * QW, QW), :] = (dot_nt(one, whole) * factor).astype(BF16)
        for j in range(4):
            factor = 0.5 if j == 3 else 1.0
            for half, part in enumerate((attn_own, attn_other)):
                attn_t[b, pl.ds(j * QW + half * 64, 64), :] = (dot_nt(small, part[b, j]) * factor).astype(BF16)
        out = jnp.concatenate([out_own[b], out_other[b]], axis=0)
        out_t[b] = (dot_nt(one, out) * 0.25).astype(BF16)
        for j in range(2):
            factor = 0.5 if j == 0 else 1.0
            for half in range(2):
                part = gateup[b, j, :, pl.ds(half * QW, QW)]
                gateup_t[b, pl.ds((2 * j + half) * QW, QW), :] = (dot_nt(one, part) * factor).astype(BF16)
        down_t[b] = (dot_nt(one, down[b]) * 0.5).astype(BF16)
        return carry

    lax.fori_loop(0, BLOCKS, block, 0)
    token_t[...] = dot_nt(one, token[...]).astype(BF16)
    high, middle, low = split(position[...])
    parts = jnp.concatenate([high, middle, low, high, middle, high], axis=0).astype(BF16)
    position_l[...] = dot_nt(one, parts).astype(BF16)
    gain_b[...] = jnp.broadcast_to(gain[...], (QW, QW))


def network(
    core_ref,
    single_own,
    single_other,
    tokens,
    rows_ref,
    bias_own,
    bias_other,
    ada,
    ada_bias,
    attn_own,
    attn_other,
    out_own,
    out_other,
    gateup,
    down,
    token,
    position,
    gain,
    final,
    result,
    ada_t,
    attn_t,
    out_t,
    gateup_t,
    down_t,
    token_t,
    position_l,
    gain_b,
    single_s,
    bias_t,
    cond_s,
    stream_s,
):
    @pl.when(pl.program_id(0) == 0)
    def _():
        prepare(
            (ada, ada_bias, attn_own, attn_other, out_own, out_other, gateup, down, token, position, gain),
            ada_t, attn_t, out_t, gateup_t, down_t, token_t, position_l, gain_b,
        )

    core = core_ref[0]
    one = eye(QW)
    wide = GROUP * QW
    own_row = pl.multiple_of(core * 64, 64)
    other_row = pl.multiple_of(64 - core * 64, 64)
    for w in range(GROUP):
        single_s[w, pl.ds(own_row, 64), :] = single_own[w]
        single_s[w, pl.ds(other_row, 64), :] = single_other[w]
        for h in range(HEADS):
            part = bias_own[h, w] if h < 2 else bias_other[h - 2, w]
            bias_t[w, h // 2, :, pl.ds((h % 2) * QW, QW)] = part.T
    rows = jnp.concatenate([rows_ref[w] for w in range(GROUP)], axis=1)
    projected = dot_nt(token_t[...], tokens[...]).astype(BF16)
    which = rows[3:4, :] + lax.broadcasted_iota(jnp.int32, (1, wide), 1) // QW * TOKW
    token_ids = lax.broadcasted_iota(jnp.int32, (GROUP * TOKW, wide), 0).astype(F32)
    one_hot = jnp.where(token_ids == which, 1.0, 0.0).astype(BF16)
    condition = dot(projected, one_hot) + jnp.concatenate(
        [dot_nt(one, single_s[w]) for w in range(GROUP)], axis=1
    )
    rest, scale = centred(condition)
    gains = jnp.concatenate([gain_b[...]] * GROUP, axis=1)
    cond_s[0:QW, :] = (rest * scale * gains).astype(BF16)
    fill = lax.broadcasted_iota(jnp.int32, (QW, wide), 0)
    cond_s[QW : 2 * QW, :] = jnp.where((fill == 0) | (fill == 8) | (fill == 16), 1.0, 0.0).astype(BF16)
    high, middle, low = split(rows)
    parts = jnp.concatenate([high, high, high, middle, middle, low], axis=0).astype(BF16)
    stream_s[...] = condition + dot(position_l[...], parts)

    def block(b, carry):
        def ada_term(j):
            return dot(ada_t[b, pl.ds(j * QW, QW), :], cond_s[...])

        stream = stream_s[...]
        rest, scale = centred(stream)
        normed = ((rest * (0.5 * scale)) * (1.0 + jnp.tanh(ada_term(0))) + ada_term(1)).astype(BF16)
        query = (dot(attn_t[b, 0:QW, :], normed) * HEAD_DIM**-0.5).astype(BF16)
        key = dot(attn_t[b, QW : 2 * QW, :], normed).astype(BF16)
        value = dot(attn_t[b, 2 * QW : 3 * QW, :], normed).astype(BF16)
        gate = 1.0 + jnp.tanh(dot(attn_t[b, 3 * QW : 4 * QW, :], normed))
        ones = jnp.ones((16, QW), BF16)
        attended = []
        for w in range(GROUP):
            lanes = slice(w * QW, (w + 1) * QW)
            left = jnp.concatenate([key[:, lanes].T, one], axis=1)
            outs = []
            for pair in range(2):
                columns = []
                for h in (2 * pair, 2 * pair + 1):
                    pieces = [jnp.zeros((HEAD_DIM, QW), BF16)] * HEADS
                    pieces[h] = query[h * HEAD_DIM : (h + 1) * HEAD_DIM, lanes]
                    columns.append(jnp.concatenate(pieces, axis=0))
                right = jnp.concatenate(
                    [jnp.concatenate(columns, axis=1), bias_t[w, pair]], axis=0
                )
                scores = dot(left, right)
                exponent = jnp.exp(scores - jnp.max(scores, axis=0, keepdims=True)).astype(BF16)
                values = jnp.concatenate([value[64 * pair : 64 * pair + 64, lanes], ones], axis=0)
                product = dot(values, exponent)
                inverse = 1.0 / product[64:65, :]
                outs.append(product[0:32, 0:QW] * inverse[:, 0:QW])
                outs.append(product[32:64, QW : 2 * QW] * inverse[:, QW : 2 * QW])
            attended.append((jnp.concatenate(outs, axis=0) * gate[:, lanes]).astype(BF16))
        update = dot(out_t[b], jnp.concatenate(attended, axis=1))
        stream = stream + update * (1.0 + jnp.tanh(ada_term(2)))
        rest, scale = centred(stream)
        normed = ((rest * (0.5 * scale)) * (1.0 + jnp.tanh(ada_term(3))) + ada_term(4)).astype(BF16)
        gate_half = dot(gateup_t[b, 0 : 2 * QW, :], normed)
        up = dot(gateup_t[b, 2 * QW : 4 * QW, :], normed)
        hidden = (gate_half * up * (1.0 + jnp.tanh(gate_half))).astype(BF16)
        stream_s[...] = stream + dot(down_t[b], hidden) * (1.0 + jnp.tanh(ada_term(5)))
        return carry

    lax.fori_loop(0, BLOCKS, block, 0)
    rest, scale = centred(stream_s[...])
    update = dot(final[...], (rest * scale).astype(BF16))
    for w in range(GROUP):
        result[w] = update[0:8, w * QW : (w + 1) * QW]


def run_network(core, single_own, single_other, tokens, rows, pair_bias, bias_other, weights, final):
    half = rows.shape[0]
    steps = half // GROUP
    hidden = weights[6].shape[-1]

    def whole(array):
        return pl.BlockSpec(array.shape, lambda s, c: (0,) * array.ndim)

    own = lambda s, c: (c[0] * steps + s, 0, 0)
    there = lambda s, c: (s, 0, 0)
    return pl.pallas_call(
        network,
        grid_spec=pltpu.PrefetchScalarGridSpec(
            num_scalar_prefetch=1,
            grid=(steps,),
            in_specs=[
                pl.BlockSpec((GROUP, QW // 2, QW), own),
                pl.BlockSpec((GROUP, QW // 2, QW), there),
                pl.BlockSpec((GROUP * TOKW, tokens.shape[1]), lambda s, c: (c[0] * steps + s, 0)),
                pl.BlockSpec((GROUP, 8, QW), there),
                pl.BlockSpec((2, GROUP, QW, QW), lambda s, c: (0, c[0] * steps + s, 0, 0)),
                pl.BlockSpec((2, GROUP, QW, QW), lambda s, c: (0, s, 0, 0)),
            ]
            + [whole(array) for array in weights]
            + [whole(final)],
            out_specs=pl.BlockSpec((GROUP, 8, QW), there),
            scratch_shapes=[
                pltpu.VMEM((BLOCKS, 6 * QW, 2 * QW), BF16),
                pltpu.VMEM((BLOCKS, 4 * QW, QW), BF16),
                pltpu.VMEM((BLOCKS, QW, QW), BF16),
                pltpu.VMEM((BLOCKS, 2 * hidden, QW), BF16),
                pltpu.VMEM((BLOCKS, QW, hidden), BF16),
                pltpu.VMEM((QW, tokens.shape[1]), BF16),
                pltpu.VMEM((QW, 48), BF16),
                pltpu.VMEM((QW, QW), F32),
                pltpu.VMEM((GROUP, QW, QW), BF16),
                pltpu.VMEM((GROUP, 2, QW, 2 * QW), BF16),
                pltpu.VMEM((2 * QW, GROUP * QW), BF16),
                pltpu.VMEM((QW, GROUP * QW), F32),
            ],
        ),
        out_shape=jax.ShapeDtypeStruct((half, 8, QW), F32),
        compiler_params=pltpu.CompilerParams(vmem_limit_bytes=48 * 1024 * 1024),
    )(core, single_own, single_other, tokens, rows, pair_bias, bias_other, *weights, final)


def local(
    coords,
    noise,
    sigma,
    atom_single,
    token_single,
    atom_token,
    window_count,
    pair_bias,
    token_weight,
    cond_gain,
    position_weight,
    ada_weight,
    ada_bias,
    attn_weight,
    out_weight,
    gateup_weight,
    down_weight,
    final_weight,
    *,
    win_total,
):
    swap = [(0, 1), (1, 0)]
    core = lax.axis_index("head")
    device_id = lax.axis_index("win")
    slot_total, quarter = atom_token.shape
    half = slot_total // 2
    first_own, first_other = core * half, (1 - core) * half

    def other_half(array, axis):
        return lax.dynamic_slice_in_dim(array, first_other, half, axis)

    def own_half(array, axis):
        return lax.dynamic_slice_in_dim(array, first_own, half, axis)

    def swapped(array):
        return lax.ppermute(array, "head", swap)

    def ordered(own, other, axis):
        return jnp.where(
            core == 0,
            jnp.concatenate([own, other], axis=axis),
            jnp.concatenate([other, own], axis=axis),
        )

    sigma_value = sigma[0]
    noisy = coords + sigma_value * noise
    live_mask = (jnp.arange(slot_total, dtype=jnp.int32) < window_count[device_id]).astype(F32)
    partial = jnp.sum(noisy * live_mask[None, :, None], axis=(1, 2))
    packed = jnp.concatenate([noisy, atom_token.astype(F32)[None]], axis=0)
    packed_other = swapped(other_half(packed, 1))
    total = jnp.zeros((8, QW), F32).at[0:3, :].set(partial[:, None])
    total = total + swapped(total)
    step = 1
    while step < win_total:
        total = total + lax.ppermute(total, "win", [(i, i ^ step) for i in range(win_total)])
        step *= 2
    centre = total[0:3, 0] / (QW * jnp.sum(window_count).astype(F32))

    bias_other = swapped(other_half(pair_bias, 1))
    single_other = swapped(other_half(atom_single, 0))
    attn_other = swapped(attn_weight)
    out_other = swapped(out_weight)

    inverse = 1.0 / (1.0 + sigma_value * sigma_value)
    rows = ordered(own_half(packed, 1), packed_other, 2)
    shifted = rows[0:3] - centre[:, None, None]
    scaled = shifted * jnp.sqrt(inverse)
    rows = jnp.concatenate([scaled, rows[3:4], jnp.zeros((4, half, QW), F32)], axis=0)
    rows = jnp.transpose(rows, (1, 0, 2))
    weights = (
        ada_weight,
        ada_bias,
        attn_weight,
        attn_other,
        out_weight,
        out_other,
        gateup_weight,
        down_weight,
        token_weight,
        jnp.zeros((8, QW), F32).at[0:3].set(position_weight),
        cond_gain.reshape(QW, 1),
    )
    final = jnp.zeros((16, QW), BF16).at[0:3].set(final_weight)
    update = run_network(
        core.reshape(1).astype(jnp.int32),
        atom_single, single_other, token_single, rows, pair_bias, bias_other, weights, final,
    )
    update = jnp.transpose(update[:, 0:3], (1, 0, 2))
    denoised = shifted * inverse + sigma_value * jnp.sqrt(inverse) * update
    denoised = denoised * own_half(live_mask, 0)[None, :, None]
    mine = lax.dynamic_slice_in_dim(denoised, core * quarter, quarter, 2)
    theirs = lax.dynamic_slice_in_dim(denoised, (1 - core) * quarter, quarter, 2)
    return ordered(mine, swapped(theirs), 1)


def solution(mesh):
    placed = (
        P(None, "win", "head"),
        P(None, "win", "head"),
        P(),
        P("win", "head", None),
        P("win", None),
        P("win", "head"),
        P(),
        P("head", "win", None, None),
        P(),
        P(),
        P(),
        P(),
        P(),
        P(None, None, None, "head"),
        P(None, "head", None),
        P(),
        P(),
        P(),
    )
    return jax.shard_map(
        functools.partial(local, win_total=mesh.shape["win"]),
        mesh=mesh,
        in_specs=placed,
        out_specs=P(None, "win", "head"),
        check_vma=False,
    )
```
